1024 devices in a mesh: row: 8 (over z_hi, core), col: 32 (over z_lo, x), tau: 4 (over y).
Axes of the slice: x: 4, y: 4, z: 32 (z_hi: 4, z_lo: 8; z = z_hi * 8 + z_lo), core: 2. Of those that a mesh axis runs over, the one named last changes fastest.
Arguments:
- occ_states: bfloat16 [8192, 512], P(('col', 'row')), may hold values from -0.25 to 0.25
- empty_states: bfloat16 [8192, 4096], P(('col', 'row')), may hold values from -0.09375 to 0.09375
- mix_weights: float32 [4096, 16], replicated, may hold values from -4 to 4
- slice_of_block: int32 [128], replicated, may hold values from 0 to 23
- occ_energy: float32 [512], replicated, may hold values from -1.2 to -0.1
- pb_energy: float32 [384], replicated, may hold values from 0.1 to 2
- tau_points: float32 [12], P('tau'), may hold values from 0.05 to 2.5
- tau_weights: float32 [12], P('tau'), may hold values from 0.05 to 0.5
- trial: bfloat16 [8192, 128], P(('col', 'row')), may hold values from -6 to 6
Outputs:
- trial_response: float32 [8192, 128], P(('col', 'row'))
The draws below stay inside these ranges and needn't reach their ends.
All inputs are finite; a program needn't handle non-finite values.
Results may differ from the reference program's by a relative error of at most 0.0018.
Values may be sent and summed in bfloat16 or wider, within the bound.
A program may use at most 32 MiB of HBM per device.

```python
import math
import jax
import jax.numpy as jnp
from jax import lax

NOCC = 512
NEMPTY = 4096
NPB = 384
PB_SLICE = 16
NV = 128
NPTS = 8192
NTAU = 12
NSLICE = 24
NEBLK = 128


def set_ends(array, key, smallest, top_value):
    place = [jax.random.randint(jax.random.fold_in(key, axis), (), 0, length) for axis, length in enumerate(array.shape)]
    widest = array.shape.index(max(array.shape))
    beside = place[:widest] + [(place[widest] + 1) % array.shape[widest]] + place[widest + 1:]
    return array.at[tuple(place)].set(smallest).at[tuple(beside)].set(top_value)


def block_levels(rng, extent, split, low, largest):
    gain, own = 1.0, jax.random.fold_in(rng, 6)
    for dim, parts in split:
        steps = jnp.exp(jax.random.uniform(jax.random.fold_in(own, dim), (parts,), jnp.float32, low / len(split), largest / len(split)))
        gain = gain * jnp.repeat(steps, extent[dim] // parts).reshape([-1 if axis == dim else 1 for axis in range(len(extent))])
    return gain


def gaussian(stream_key, extent, deviation, limit, cuts=(), kind=jnp.bfloat16):
    array = jax.random.normal(stream_key, extent, jnp.float32) * deviation
    if len(cuts) > 0:
        array = block_levels(stream_key, extent, cuts, -0.22, 0.18) * array
    return jnp.clip(array, min=-limit, max=limit).astype(kind)


def setup_inputs(seed: int = 0) -> dict:
    seeds = jax.random.split(jax.random.key(seed), 10)
    occ_states = gaussian(seeds[0], (NPTS, NOCC), NOCC ** -0.5, 0.25, ((0, 256),))
    empty_states = gaussian(seeds[1], (NPTS, NEMPTY), NEMPTY ** -0.5, 0.09375, ((0, 256),))
    mix_weights = gaussian(seeds[2], (NEMPTY, PB_SLICE), 1.0, 4.0, (), jnp.float32)
    slice_of_block = set_ends(jax.random.randint(seeds[3], (NEBLK,), 0, NSLICE), jax.random.fold_in(seeds[3], 1), 0, NSLICE - 1).astype(jnp.int32)
    occ_energy = jnp.clip(jax.random.uniform(seeds[4], (NOCC,), jnp.float32, -1.2, -0.1), -1.2, -0.1)
    pb_energy = jnp.clip(jnp.exp(jax.random.uniform(seeds[5], (NPB,), jnp.float32, math.log(0.1), math.log(2.0))), 0.1, 2.0)
    tau_points = jnp.clip(jnp.exp(math.log(2.5) - 3.912023 * jax.random.uniform(seeds[6], (NTAU,), jnp.float32) ** block_levels(seeds[6], (NTAU,), ((0, 4),), -0.2, 0.2)), 0.05, 2.5)
    tau_weights = jnp.clip(jnp.exp(math.log(0.5) - 2.3025851 * jax.random.uniform(seeds[7], (NTAU,), jnp.float32) ** block_levels(seeds[7], (NTAU,), ((0, 4),), -0.2, 0.2)), 0.05, 0.5)
    trial = gaussian(seeds[8], (NPTS, NV), 1.0, 6.0, ((0, 256),))
    return {"occ_states": occ_states, "empty_states": empty_states, "mix_weights": mix_weights, "slice_of_block": slice_of_block, "occ_energy": occ_energy, "pb_energy": pb_energy, "tau_points": tau_points, "tau_weights": tau_weights, "trial": trial}


def mixing_matrix(mix_weights, slice_of_block, nbands):
    per_slice = mix_weights.shape[1]
    state_slice = jnp.repeat(slice_of_block, mix_weights.shape[0] // slice_of_block.shape[0])
    band_slice = jnp.arange(nbands, dtype=jnp.int32) // per_slice
    picked = state_slice[:, None] == band_slice[None, :]
    spread_weights = jnp.tile(mix_weights, (1, nbands // per_slice))
    return jnp.where(picked, spread_weights, jnp.zeros_like(spread_weights)).astype(jnp.bfloat16)


def contract(left, right):
    return lax.dot_general(left, right, (((1,), (1,)), ((), ())), preferred_element_type=jnp.float32)


def reference(occ_states, empty_states, mix_weights, slice_of_block, occ_energy, pb_energy, tau_points, tau_weights, trial):
    band_mix = mixing_matrix(mix_weights, slice_of_block, NPB)
    pseudo = jnp.dot(empty_states, band_mix, preferred_element_type=jnp.float32).astype(jnp.bfloat16)
    occ_wide = occ_states.astype(jnp.float32)
    pb_wide = pseudo.astype(jnp.float32)
    block_rows = math.gcd(NPTS, 1024)
    block_count = NPTS // block_rows
    row_occ = occ_states.reshape(block_count, block_rows, NOCC)
    row_pb = pseudo.reshape(block_count, block_rows, NPB)

    def one_block(row_pieces):
        rows_occ, rows_pb = row_pieces

        def one_time(summed, entries):
            time_point, weight = entries
            occ_scaled = (occ_wide * jnp.exp(occ_energy * time_point)[None, :]).astype(jnp.bfloat16)
            pb_scaled = (pb_wide * jnp.exp(-pb_energy * time_point)[None, :]).astype(jnp.bfloat16)
            g_occ = contract(rows_occ, occ_scaled)
            g_un = contract(rows_pb, pb_scaled)
            chi_tile = (weight * g_occ * g_un).astype(jnp.bfloat16)
            return summed + jnp.dot(chi_tile, trial, preferred_element_type=jnp.float32), None

        summed, _ = lax.scan(one_time, jnp.zeros((block_rows, NV), jnp.float32), (tau_points, tau_weights))
        return summed

    responses = lax.map(one_block, (row_occ, row_pb))
    return responses.reshape(NPTS, NV)
```

```python
import functools

import jax
import jax.numpy as jnp
from jax import lax
from jax.experimental import pallas as pl
from jax.experimental.pallas import tpu as pltpu
from jax.sharding import PartitionSpec as P

MESH = pl.DeviceIdType.MESH

NX, NY, NZ, NCORE = 4, 4, 32, 2
STRIDE = 4
RING = NZ // STRIDE
NBLK = NX * NCORE
NEAR = 2 * (STRIDE - 1)
CHUNKS, LANES = 4, 256


def kernel(
    occ, empty, mix_t, block_slice, occ_energy, pb_energy, tau, weight, trial, out,
    rows, cols, empty_v, mix_v, band_mix, times, decay, lane_weight, total, parts, tau_parts,
    load_sem, right_sem, left_sem, near_sem, cols_sem, rows_send, rows_recv,
    times_send, times_recv, part_send, part_recv, tau_send, tau_recv,
):
    row, col, y = lax.axis_index("row"), lax.axis_index("col"), lax.axis_index("tau")
    core, x = lax.rem(row, 2), lax.rem(col, NX)
    z = 8 * lax.div(row, 2) + lax.div(col, NX)
    npts = occ.shape[0]
    ntau = tau.shape[0]

    def device(x, y, z, core):
        return (2 * lax.div(z, 8) + core, NX * lax.rem(z, 8) + x, y)

    def copy(src, dst, send, recv, target):
        return pltpu.make_async_remote_copy(
            src_ref=src, dst_ref=dst, send_sem=send, recv_sem=recv,
            device_id=target, device_id_type=MESH,
        )

    def place(z):
        stop = lax.div(z, STRIDE)
        first = 2 * lax.rem(lax.rem(z, STRIDE) - y + STRIDE, STRIDE)
        return stop, first, lax.rem(stop - first + RING, RING)

    def neighbour(n):
        return lax.rem(z + (1 - 2 * (n % 2)) * (STRIDE - 1 - n // 2) + NZ, NZ)

    stop, first, ahead = place(z)
    right = device(x, y, lax.rem(z + STRIDE, NZ), core)
    left = device(x, y, lax.rem(z + NZ - STRIDE, NZ), core)
    near = [device(x, y, neighbour(n), core) for n in range(NEAR)]
    at_source = 1 - lax.div(ahead + RING - 2, RING)
    given = 1 - lax.rem(stop, 2)

    def hops_right(b):
        return lax.rem(stop - first - b + RING, RING)

    def hops_left(b):
        return lax.rem(first + b - stop + RING, RING)

    me = NCORE * x + core
    peers = []
    for dx in range(NX):
        for dc in range(NCORE):
            if dx + dc > 0:
                px, pc = lax.rem(x + dx, NX), lax.rem(core + dc, NCORE)
                peers.append((NCORE * px + pc, device(px, y, z, pc)))
    tau_peers = []
    for dy in range(1, NY):
        py = lax.rem(y + dy, NY)
        tau_peers.append((py, device(x, py, z, core)))

    loads = [
        pltpu.make_async_copy(occ.at[:, 0:256], rows.at[me, 0], load_sem.at[0]),
        pltpu.make_async_copy(occ.at[:, 256:512], rows.at[me, 1], load_sem.at[1]),
        pltpu.make_async_copy(trial, rows.at[me, 3, :, 128:256], load_sem.at[2]),
        pltpu.make_async_copy(empty, empty_v, load_sem.at[3]),
        pltpu.make_async_copy(mix_t, mix_v, load_sem.at[4]),
    ]
    for load in loads:
        load.start()

    barrier = pltpu.get_barrier_semaphore()
    everyone = [right, left, *near, *[p[1] for p in peers], *[p[1] for p in tau_peers]]
    for target in everyone:
        pl.semaphore_signal(barrier, inc=1, device_id=target, device_id_type=MESH)

    for i in range(ntau):
        times[y, pl.ds(i, 1), :] = jnp.full((1, 128), tau[i], jnp.float32)
        times[y, pl.ds(ntau + i, 1), :] = jnp.full((1, 128), weight[i], jnp.float32)

    def chain_sends(b, c, source):
        dst, recv = cols.at[first + b, c], cols_sem.at[first + b, c]
        to_right = copy(source, dst, right_sem.at[b, c], recv, right)
        to_left = copy(source, dst, left_sem.at[b, c], recv, left)
        return to_right, to_left

    def near_sends(b, c, source):
        dst, recv = cols.at[first + b, c], cols_sem.at[first + b, c]
        return [copy(source, dst, near_sem.at[n, c], recv, t) for n, t in enumerate(near)]

    def pass_on(b, c, source):
        to_right, to_left = chain_sends(b, c, source)
        pl.when(hops_right(b) < RING // 2)(to_right.start)
        pl.when(hops_left(b) < RING // 2 - 1)(to_left.start)

    def send_own(half):
        @pl.when(at_source == 1)
        def _():
            for c in (2 * half, 2 * half + 1):
                pass_on(ahead, c, rows.at[me, c])

        for n, (_, target) in enumerate(peers):
            piece = rows.at[me, pl.ds(2 * half, 2)]
            copy(piece, piece, rows_send.at[n, half], rows_recv.at[me, half], target).start()

    loads[4].wait()
    per_slice = mix_t.shape[0]
    lane = lax.broadcasted_iota(jnp.int32, (per_slice, 128), 1)
    states = empty.shape[1] // block_slice.shape[0]
    per_tile = 128 // states

    def mix_tile(t, carry):
        picked = jnp.full((per_slice, 128), block_slice[per_tile * t], jnp.int32)
        for i in range(1, per_tile):
            here = block_slice[per_tile * t + i]
            picked = jnp.where(lane >= states * i, here, picked)
        lanes = pl.ds(pl.multiple_of(128 * t, 128), 128)
        values = mix_v[:, lanes]
        for s in range(band_mix.shape[0] // per_slice):
            band_mix[s * per_slice : (s + 1) * per_slice, lanes] = jnp.where(
                picked == s, values, 0.0
            ).astype(jnp.bfloat16)
        return carry

    lax.fori_loop(0, empty.shape[1] // 128, mix_tile, 0)
    loads[3].wait()
    pseudo = lax.dot_general(
        empty_v[...], band_mix[...], (((1,), (1,)), ((), ())), preferred_element_type=jnp.float32
    ).astype(jnp.bfloat16)
    loads[2].wait()
    rows[me, 2] = pseudo[:, 0:256]
    rows[me, 3, :, 0:128] = pseudo[:, 256:384]
    loads[0].wait()
    loads[1].wait()
    pl.semaphore_wait(barrier, len(everyone))
    send_own(0)
    send_own(1)
    for n, (_, target) in enumerate(tau_peers):
        copy(times.at[y], times.at[y], times_send.at[n], times_recv.at[y], target).start()

    keep = pltpu.make_async_copy(rows.at[me], cols.at[stop], load_sem.at[5])
    pl.when(at_source == 1)(keep.start)

    for _, (py, target) in enumerate(tau_peers):
        copy(times.at[y], times.at[py], times_send.at[0], times_recv.at[py], target).wait_recv()
    ranks = [(k // ntau, k % ntau) for k in range(NY * ntau)]
    occ_row = occ_energy[...].reshape(1, 512)
    pb_row = pb_energy[...].reshape(1, 384)
    for k, (ky, ki) in enumerate(ranks):
        point = times[ky, ki : ki + 1, :]
        point4 = jnp.concatenate([point] * 4, axis=1)
        decay[k : k + 1, 0:512] = jnp.exp(occ_row * point4)
        decay[k : k + 1, 512:896] = jnp.exp(-pb_row * point4[:, 0:384])
    lane_row = lax.broadcasted_iota(jnp.int32, (1, 128), 1)
    per_lanes = 128 // npts
    for g in range(len(ranks) // per_lanes):
        spread = None
        for i in range(per_lanes):
            ky, ki = ranks[g * per_lanes + i]
            here = times[ky, ntau + ki : ntau + ki + 1, :]
            spread = here if spread is None else jnp.where(lane_row >= npts * i, here, spread)
        lane_weight[:, 128 * g : 128 * (g + 1)] = spread

    total[...] = jnp.zeros_like(total)

    def columns(slot):
        def product(c, lanes):
            left_side = rows[:, c, :, 0:lanes].reshape(NBLK * npts, lanes)
            points = cols[slot, c, :, 0:lanes].astype(jnp.float32)
            scaled = jnp.concatenate(
                [
                    (points * decay[k : k + 1, LANES * c : LANES * c + lanes]).astype(jnp.bfloat16)
                    for k in range(len(ranks))
                ],
                axis=0,
            )
            return lax.dot_general(
                left_side, scaled, (((1,), (1,)), ((), ())), preferred_element_type=jnp.float32
            )

        g_occ = product(0, 256) + product(1, 256)
        g_un = product(2, 256) + product(3, 128)
        chi = (lane_weight[...] * g_occ * g_un).astype(jnp.bfloat16)
        vectors = jnp.concatenate([cols[slot, 3, :, 128:256]] * len(ranks), axis=0)
        total[...] += jnp.dot(chi, vectors, preferred_element_type=jnp.float32)

    def arrived(slot, c):
        copy(
            cols.at[slot, c], cols.at[slot, c], right_sem.at[0, c], cols_sem.at[slot, c], right
        ).wait_recv()

    early = 1 - lax.div(ahead, 5)

    def event(i, carry):
        turn, c = lax.div(i, CHUNKS), lax.rem(i, CHUNKS)
        b = turn * (1 - early) + (1 - turn) * early

        @pl.when(b != ahead)
        def _():
            source = cols.at[first + b, c]
            arrived(first + b, c)
            pass_on(b, c, source)

            @pl.when(b == given)
            def _():
                for send in near_sends(b, c, source):
                    send.start()

        return carry

    lax.fori_loop(0, 2 * CHUNKS, event, 0)
    for n, (block, target) in enumerate(peers):
        for half in range(2):
            piece = rows.at[block, pl.ds(2 * half, 2)]
            copy(piece, piece, rows_send.at[n, half], rows_recv.at[block, half], target).wait_recv()
    pl.when(at_source == 1)(keep.wait)

    def chain_columns(b, carry):
        columns(first + b)
        return carry

    lax.fori_loop(0, 2, chain_columns, 0)

    def near_columns(t, carry):
        turn, n = lax.div(t, NEAR), lax.rem(t, NEAR)
        there = lax.rem(
            z + (1 - 2 * lax.rem(n, 2)) * (STRIDE - 1 - lax.div(n, 2)) + NZ, NZ
        )
        its_stop, its_first, its_ahead = place(there)

        @pl.when(lax.div(lax.rem(its_ahead + 1, RING), 4) == turn)
        def _():
            slot = its_first + 1 - lax.rem(its_stop, 2)
            for c in range(CHUNKS):
                arrived(slot, c)
            columns(slot)

        return carry

    lax.fori_loop(0, 2 * NEAR, near_columns, 0)

    for n, (block, target) in enumerate(peers):
        copy(
            total.at[pl.ds(block * npts, npts)], parts.at[me], part_send.at[n], part_recv.at[me], target
        ).start()
    parts[me] = total[pl.ds(pl.multiple_of(me * npts, npts), npts), :]
    for n, (block, target) in enumerate(peers):
        copy(
            total.at[pl.ds(block * npts, npts)], parts.at[block], part_send.at[n], part_recv.at[block], target
        ).wait()
    summed = parts[0]
    for b in range(1, NBLK):
        summed += parts[b]
    tau_parts[y] = summed
    for n, (py, target) in enumerate(tau_peers):
        copy(tau_parts.at[y], tau_parts.at[y], tau_send.at[n], tau_recv.at[y], target).start()
    for n, (py, target) in enumerate(tau_peers):
        copy(tau_parts.at[y], tau_parts.at[py], tau_send.at[n], tau_recv.at[py], target).wait()
    answer = tau_parts[0]
    for k in range(1, NY):
        answer += tau_parts[k]
    out[...] = answer

    def left_behind(i, carry):
        b, c = lax.div(i, CHUNKS), lax.rem(i, CHUNKS)
        source = cols.at[first + b, c]
        to_right, to_left = chain_sends(b, c, source)
        pl.when(hops_right(b) < RING // 2)(to_right.wait_send)
        pl.when(hops_left(b) < RING // 2 - 1)(to_left.wait_send)

        @pl.when(b == given)
        def _():
            for send in near_sends(b, c, source):
                send.wait_send()

        return carry

    lax.fori_loop(0, 2 * CHUNKS, left_behind, 0)
    for n, (_, target) in enumerate(peers):
        for half in range(2):
            piece = rows.at[me, pl.ds(2 * half, 2)]
            copy(piece, piece, rows_send.at[n, half], rows_recv.at[me, half], target).wait_send()
    for n, (_, target) in enumerate(tau_peers):
        copy(times.at[y], times.at[y], times_send.at[n], times_recv.at[y], target).wait_send()


def local(
    occ_states,
    empty_states,
    mix_weights,
    slice_of_block,
    occ_energy,
    pb_energy,
    tau_points,
    tau_weights,
    trial,
):
    npts, nvec = trial.shape
    nempty, npb, nocc = empty_states.shape[1], pb_energy.shape[0], occ_energy.shape[0]
    ntime = NY * tau_points.shape[0]
    anywhere = pl.BlockSpec(memory_space=pl.ANY)
    vector = pl.BlockSpec(memory_space=pltpu.VMEM)
    scalar = pl.BlockSpec(memory_space=pltpu.SMEM)
    dma = pltpu.SemaphoreType.DMA
    flops = 2 * (NBLK * npts) ** 2 * ntime * (nocc + npb + nvec)
    return pl.pallas_call(
        kernel,
        out_shape=jax.ShapeDtypeStruct((npts, nvec), jnp.float32),
        in_specs=[anywhere, anywhere, anywhere, scalar, vector, vector, scalar, scalar, anywhere],
        out_specs=vector,
        scratch_shapes=[
            pltpu.VMEM((NBLK, CHUNKS, npts, LANES), jnp.bfloat16),
            pltpu.VMEM((NBLK, CHUNKS, npts, LANES), jnp.bfloat16),
            pltpu.VMEM((npts, nempty), jnp.bfloat16),
            pltpu.VMEM((mix_weights.shape[1], nempty), jnp.float32),
            pltpu.VMEM((npb, nempty), jnp.bfloat16),
            pltpu.VMEM((NY, 8, 128), jnp.float32),
            pltpu.VMEM((16, CHUNKS * LANES), jnp.float32),
            pltpu.VMEM((1, ntime * npts), jnp.float32),
            pltpu.VMEM((NBLK * npts, nvec), jnp.float32),
            pltpu.VMEM((NBLK, npts, nvec), jnp.float32),
            pltpu.VMEM((NY, npts, nvec), jnp.float32),
            dma((6,)),
            dma((2, CHUNKS)),
            dma((2, CHUNKS)),
            dma((NEAR, CHUNKS)),
            dma((NBLK, CHUNKS)),
            dma((NBLK - 1, 2)),
            dma((NBLK, 2)),
            dma((NY - 1,)),
            dma((NY,)),
            dma((NBLK - 1,)),
            dma((NBLK,)),
            dma((NY - 1,)),
            dma((NY,)),
        ],
        compiler_params=pltpu.CompilerParams(
            collective_id=0, has_side_effects=True, vmem_limit_bytes=63 << 20
        ),
        cost_estimate=pl.CostEstimate(flops=flops, bytes_accessed=1 << 21, transcendentals=1 << 14),
        name="rpa_response",
    )(
        occ_states,
        empty_states,
        mix_weights.T,
        slice_of_block,
        occ_energy,
        pb_energy,
        tau_points,
        tau_weights,
        trial,
    )


def solution(mesh):
    in_specs = (
        P(("col", "row"), None),
        P(("col", "row"), None),
        P(),
        P(),
        P(),
        P(),
        P("tau"),
        P("tau"),
        P(("col", "row"), None),
    )
    out_specs = P(("col", "row"), None)
    return jax.shard_map(local, mesh=mesh, in_specs=in_specs, out_specs=out_specs, check_vma=False)
```
